32 devices in a mesh: groups: 2 (over y), owner: 4 (over z), sub: 2 (over x), pair: 2 (over core).
Axes of the slice: x: 2, y: 2, z: 4, core: 2. Of those that a mesh axis runs over, the one named last changes fastest.
Arguments:
- embeddings: float32 [16, 2, 128, 1152], P(('groups', 'owner', 'sub'), 'pair'), parts along dimension 0, may hold values from -12 to 12
- moves: int32 [2, 16, 2, 128], P(None, ('groups', 'owner', 'sub'), 'pair'), parts along dimension 1, may hold values from -1 to 7, as said below
Outputs:
- curated: float32 [16, 2, 128, 1152], P(('groups', 'owner', 'sub'), 'pair'), parts along dimension 0
The draws below stay inside these ranges and needn't reach their ends.
There are 2 independent parts, one for each index of `groups`. The reference program is written for one: setup_inputs(seed, part) draws one part's arguments, and reference() takes and returns one part's arrays. A program takes and returns all parts, laid end to end along the dimension named above; each array names one. Nothing has to cross between parts.
Inputs may be any that keep to these rules, and one draw needn't show every extreme that they name: moves[m, c, p, s] is the cluster to which the row in slot s of device (c, p) goes after pass m + 1, or -1 for an empty slot; the row stays on pair index p. A device's live slots come first. In one list at most 16 live rows of one device go to one cluster, and some device sends 16 to every cluster; some device holds 128 live rows and some device receives 128, in every list. The live slots of a device in list m + 1 number exactly the rows it receives from list m.
All inputs are finite; a program needn't handle non-finite values.
Results may differ from the reference program's by a relative error of at most 0.002.
Values may be sent and summed in bfloat16 or wider, within the bound.
No kernel may reach another device: no remote copies, remote signals or barrier semaphores. Data moves between devices by JAX's collectives and lax.ppermute only.
A program may use at most 64 MiB of HBM per device.

```python
import jax
import jax.numpy as jnp
from jax import lax

D = 1152
ROWS_DEV = 128
PASSES = 3
MIGRATIONS = 2
CLUSTERS = 8
SHARES = 2
MOST = 16


def draw_embeddings(key, part):
    key_modes, key_centers, key_noise = jax.random.split(key, 3)
    shape = (CLUSTERS, SHARES, ROWS_DEV, D)
    modes = jax.random.randint(key_modes, (CLUSTERS, SHARES, ROWS_DEV), 0, 16)
    centers = jax.random.normal(key_centers, (16, D), jnp.float32)
    base = centers[modes]
    noise = jax.random.normal(key_noise, shape, jnp.float32)
    values = 0.9 * base + noise
    return jnp.clip(values, -12.0, 12.0).astype(jnp.float32)


def first_traffic(key):
    key_raw, key_limit, key_row, key_col = jax.random.split(key, 4)
    raw_counts = jax.random.randint(key_raw, (CLUSTERS, CLUSTERS), MOST // 2, MOST + 1)
    limits = jax.random.randint(key_limit, (CLUSTERS,), min(2, MOST), MOST + 1)
    traffic = jnp.minimum(raw_counts, limits[None, :])
    full_row = jax.random.randint(key_row, (), 0, CLUSTERS)
    full_col = jax.random.randint(key_col, (), 0, CLUSTERS)
    cluster_ids = jnp.arange(CLUSTERS, dtype=jnp.int32)
    forced = (cluster_ids[:, None] == full_row) | (cluster_ids[None, :] == full_col)
    return jnp.where(forced, MOST, traffic).astype(jnp.int32)


def slot_list(key, counts_row):
    ends = jnp.cumsum(counts_row)
    total = ends[-1]
    slot_ids = jnp.arange(ROWS_DEV, dtype=jnp.int32)
    sequence = jnp.sum((ends[None, :] <= slot_ids[:, None]).astype(jnp.int32), axis=1)
    sequence = jnp.where(slot_ids < total, sequence, -1)
    random_part = jax.random.randint(key, (ROWS_DEV,), 0, 2 ** 20)
    sort_keys = jnp.where(slot_ids < total, random_part * ROWS_DEV + slot_ids, 2 ** 30 + slot_ids)
    order = jnp.argsort(sort_keys)
    return sequence[order].astype(jnp.int32)


def share_moves(key):
    key_list = jax.random.split(key, 2 * MIGRATIONS + 1)
    traffic = first_traffic(key_list[0])
    lists = []
    for number in range(MIGRATIONS):
        slot_keys = jax.random.split(key_list[2 * number + 1], CLUSTERS)
        lists.append(jax.vmap(slot_list)(slot_keys, traffic))
        shuffle = jax.random.permutation(key_list[2 * number + 2], CLUSTERS)
        traffic = traffic.T[:, shuffle]
    return jnp.stack(lists)


def draw_moves(key, part):
    per_share = jax.vmap(share_moves)(jax.random.split(jax.random.fold_in(key, 7), SHARES))
    return jnp.transpose(per_share, (1, 2, 0, 3)).astype(jnp.int32)


def setup_inputs(seed: int = 0, part: int = 0) -> dict:
    keys = jax.random.split(jax.random.key(seed), 3)
    part_splits = jax.random.split(jax.random.fold_in(keys[2], part), 3)
    return {
        "embeddings": draw_embeddings(jax.random.fold_in(jax.random.fold_in(keys[2], part), 71), part),
        "moves": draw_moves(jax.random.fold_in(jax.random.fold_in(keys[2], part), 71), part),
    }


epsilon = 1e-06
sharpness = 6.0

def unit_rows(values):
    return values / jnp.sqrt(lax.optimization_barrier(jnp.sum(values * values, axis=-1, keepdims=True)) + epsilon)

def shift_cluster(pieces):
    rows, marks = pieces
    key_rows = rows.reshape(SHARES * ROWS_DEV, D)
    key_live = marks.reshape(SHARES * ROWS_DEV)
    scores = jnp.dot(key_rows, key_rows.T, preferred_element_type=jnp.float32)
    weights = jnp.where(key_live[None, :], jnp.exp(sharpness * (scores - 1.0)), 0.0).astype(jnp.bfloat16)
    numer = jnp.dot(weights, key_rows, preferred_element_type=jnp.float32)
    denom = lax.optimization_barrier(jnp.sum(weights.astype(jnp.float32), axis=1))
    shifted = numer / jnp.where(key_live, denom, 1.0)[:, None]
    result = jnp.where(key_live[:, None], unit_rows(shifted), 0.0)
    return result.reshape(SHARES, ROWS_DEV, D)

def migrate_share(rows, targets):
    flat_rows = rows.reshape(CLUSTERS * ROWS_DEV, D)
    flat_targets = jnp.where(targets >= 0, targets, CLUSTERS).reshape(CLUSTERS * ROWS_DEV).astype(jnp.int32)
    order = jnp.argsort(flat_targets, stable=True).astype(jnp.int32)
    sorted_targets = flat_targets[order]
    counts = jnp.bincount(flat_targets, length=CLUSTERS + 1).astype(jnp.int32)
    starts = (jnp.cumsum(counts) - counts).astype(jnp.int32)
    ranks = jnp.arange(CLUSTERS * ROWS_DEV, dtype=jnp.int32) - starts[sorted_targets]
    places = (sorted_targets * ROWS_DEV + ranks).astype(jnp.int32)
    moved = jnp.zeros_like(flat_rows).at[places].set(flat_rows[order], mode='drop')
    flags = jnp.zeros((CLUSTERS * ROWS_DEV,), jnp.int32).at[places].set(1, mode='drop')
    return (moved.reshape(CLUSTERS, ROWS_DEV, D), flags.reshape(CLUSTERS, ROWS_DEV) > 0)

def migrate(state, targets):
    moved_all = []
    flags_all = []
    for share in range(SHARES):
        moved, flags = migrate_share(state[:, share], targets[:, share])
        moved_all.append(moved)
        flags_all.append(flags)
    return (jnp.stack(moved_all, axis=1), jnp.stack(flags_all, axis=1))

def reference(embeddings, moves):
    live_mask = moves[0] >= 0
    state = jnp.where(live_mask[..., None], unit_rows(embeddings), 0.0).astype(jnp.bfloat16)
    result = jnp.zeros(embeddings.shape, jnp.float32)
    for number in range(PASSES):
        result = lax.map(shift_cluster, (state, live_mask))
        if number + 1 < PASSES:
            state, live_mask = migrate(result.astype(jnp.bfloat16), moves[number])
    return result
```

```python
import jax
import jax.numpy as jnp
from jax import lax
from jax.experimental import pallas as pl
from jax.experimental.pallas import tpu as pltpu
from jax.sharding import PartitionSpec as P

PASSES = 3
LANES = 128
MARK = 2.0

epsilon = 1e-06
sharpness = 6.0

f32 = jnp.float32
bf16 = jnp.bfloat16


def mark_empty(block, filled):
    lane = lax.broadcasted_iota(jnp.int32, block.shape, 1)
    return jnp.where((lane == 0) & (filled < 0.5), MARK, block)


def state_kernel(emb_ref, moves_ref, out_ref):
    rows = emb_ref.shape[0]
    values = emb_ref[...]
    count = jnp.sum((moves_ref[0:1, :] >= 0).astype(f32), axis=1, keepdims=True)
    slot = lax.broadcasted_iota(jnp.int32, (rows, LANES), 0).astype(f32)
    live = (slot < count).astype(f32)
    total = jnp.sum(values * values, axis=1, keepdims=True)
    unit = values * lax.rsqrt(total + epsilon)
    unit = jnp.where(live[:, 0:1] > 0.5, unit, 0.0)
    out_ref[:, LANES:] = unit[:, LANES:].astype(bf16)
    out_ref[:, :LANES] = mark_empty(unit[:, :LANES], live).astype(bf16)


def places_kernel(clusters, most, moves_ref, out_ref):
    lists, rows = moves_ref.shape
    before = lax.broadcasted_iota(jnp.int32, (rows, rows), 0) < lax.broadcasted_iota(
        jnp.int32, (rows, rows), 1
    )
    before = before.astype(bf16)
    cluster = lax.broadcasted_iota(jnp.int32, (clusters, rows), 0)
    for number in range(lists):
        targets = moves_ref[number : number + 1, :]
        onehot = (cluster == targets).astype(f32)
        earlier = jnp.dot(onehot.astype(bf16), before, preferred_element_type=f32)
        rank = jnp.sum(onehot * earlier, axis=0, keepdims=True)
        place = targets * most + rank.astype(jnp.int32)
        out_ref[number : number + 1, :] = jnp.where(targets >= 0, place, -1)


def pass_kernel(compact, last, number, own_ref, peer_ref, places_ref, out_ref):
    rows, width = own_ref.shape

    def cleaned(ref):
        head = ref[:, :LANES].astype(f32)
        live = (head[:, 0:1] < 1.5).astype(f32)
        live = jnp.broadcast_to(live, (rows, LANES))
        head = jnp.where(live > 0.5, head, 0.0)
        return jnp.concatenate(
            [head.astype(bf16), ref[:, LANES:], live.astype(bf16)], axis=1
        ), live

    own, own_live = cleaned(own_ref)
    peer, _ = cleaned(peer_ref)
    keys = jnp.concatenate([own, peer], axis=0)
    if compact:
        row = lax.broadcasted_iota(jnp.int32, (rows, rows), 0)
        col = lax.broadcasted_iota(jnp.int32, (rows, rows), 1)
        dest = jnp.dot(
            (col < row).astype(bf16), own_live.astype(bf16), preferred_element_type=f32
        )
        slots = lax.broadcasted_iota(jnp.int32, (rows, LANES), 1).astype(f32)
        select = ((dest == slots) & (own_live > 0.5)).astype(bf16)
        query = lax.dot_general(
            select, own, (((0,), (0,)), ((), ())), preferred_element_type=f32
        )
        query_live = query[:, width:]
        query = query[:, :width].astype(bf16)
    else:
        query_live = own_live
        query = own[:, :width]
    scores = lax.dot_general(
        query, keys[:, :width], (((1,), (1,)), ((), ())), preferred_element_type=f32
    )
    weights = jnp.exp(sharpness * (scores - 1.0)).astype(bf16)
    sums = jnp.dot(weights, keys, preferred_element_type=f32)
    numer = sums[:, :width]
    inverse = 1.0 / sums[:, width : width + 1]
    total = jnp.sum(numer * numer, axis=1, keepdims=True)
    scale = inverse * lax.rsqrt(total * (inverse * inverse) + epsilon)
    unit = jnp.where(query_live[:, 0:1] > 0.5, numer * scale, 0.0)
    if last:
        out_ref[...] = unit
        return
    place = places_ref[number : number + 1, :]
    wanted = lax.broadcasted_iota(jnp.int32, (rows, rows), 0)
    choose = (wanted == place).astype(bf16)
    filled = jnp.sum(choose.astype(f32), axis=1, keepdims=True)
    outgoing = jnp.dot(choose, unit.astype(bf16), preferred_element_type=f32)
    out_ref[:, LANES:] = outgoing[:, LANES:].astype(bf16)
    out_ref[:, :LANES] = mark_empty(outgoing[:, :LANES], filled).astype(bf16)


def call(kernel, out, *args):
    spec = pl.BlockSpec(memory_space=pltpu.VMEM)
    return pl.pallas_call(
        kernel, out_shape=out, in_specs=[spec] * len(args), out_specs=spec
    )(*args)


def swap_pair(values):
    return lax.ppermute(values, "pair", [(0, 1), (1, 0)])


def body(embeddings, moves):
    rows, width = embeddings.shape[2:]
    clusters = lax.axis_size("owner") * lax.axis_size("sub")
    most = rows // clusters
    targets = moves[:, 0, 0, :]
    state = call(
        state_kernel, jax.ShapeDtypeStruct((rows, width), bf16), embeddings[0, 0], targets
    )
    places = call(
        lambda *refs: places_kernel(clusters, most, *refs),
        jax.ShapeDtypeStruct(targets.shape, jnp.int32),
        targets,
    )
    for number in range(PASSES):
        last = number + 1 == PASSES
        peer = swap_pair(state)
        result = call(
            lambda *refs: pass_kernel(number > 0, last, number, *refs),
            jax.ShapeDtypeStruct((rows, width), f32 if last else bf16),
            state,
            peer,
            places,
        )
        if not last:
            state = lax.all_to_all(
                result.reshape(clusters, most, width),
                ("owner", "sub"),
                split_axis=0,
                concat_axis=0,
                tiled=True,
            ).reshape(rows, width)
    return result[None, None]


def solution(mesh):
    placed = (
        P(("groups", "owner", "sub"), "pair", None, None),
        P(None, ("groups", "owner", "sub"), "pair", None),
    )
    return jax.shard_map(
        body,
        mesh=mesh,
        in_specs=placed,
        out_specs=P(("groups", "owner", "sub"), "pair", None, None),
        check_vma=False,
    )
```

```python
import jax
import jax.numpy as jnp
from jax import lax
from jax.experimental import pallas as pl
from jax.experimental.pallas import tpu as pltpu
from jax.sharding import PartitionSpec as P

PASSES = 3
LANES = 128
MARK = 2.0

epsilon = 1e-06
sharpness = 6.0

f32 = jnp.float32
bf16 = jnp.bfloat16


def mark_empty(block, filled):
    lane = lax.broadcasted_iota(jnp.int32, block.shape, 1)
    return jnp.where((lane == 0) & (filled < 0.5), MARK, block)


def state_kernel(emb_ref, moves_ref, out_ref):
    rows = emb_ref.shape[0]
    values = emb_ref[...]
    count = jnp.sum((moves_ref[0:1, :] >= 0).astype(f32), axis=1, keepdims=True)
    slot = lax.broadcasted_iota(jnp.int32, (rows, LANES), 0).astype(f32)
    live = (slot < count).astype(f32)
    total = jnp.sum(values * values, axis=1, keepdims=True)
    unit = values * lax.rsqrt(total + epsilon)
    unit = jnp.where(live[:, 0:1] > 0.5, unit, 0.0)
    out_ref[:, LANES:] = unit[:, LANES:].astype(bf16)
    out_ref[:, :LANES] = mark_empty(unit[:, :LANES], live).astype(bf16)


def places_kernel(clusters, most, moves_ref, out_ref):
    lists, rows = moves_ref.shape
    before = lax.broadcasted_iota(jnp.int32, (rows, rows), 0) < lax.broadcasted_iota(
        jnp.int32, (rows, rows), 1
    )
    before = before.astype(bf16)
    cluster = lax.broadcasted_iota(jnp.int32, (clusters, rows), 0)
    for number in range(lists):
        targets = moves_ref[number : number + 1, :]
        onehot = (cluster == targets).astype(f32)
        earlier = jnp.dot(onehot.astype(bf16), before, preferred_element_type=f32)
        rank = jnp.sum(onehot * earlier, axis=0, keepdims=True)
        place = targets * most + rank.astype(jnp.int32)
        out_ref[number : number + 1, :] = jnp.where(targets >= 0, place, -1)


def pass_kernel(compact, last, number, own_ref, peer_ref, places_ref, out_ref):
    rows, width = own_ref.shape

    def cleaned(ref):
        head = ref[:, :LANES].astype(f32)
        live = (head[:, 0:1] < 1.5).astype(f32)
        live = jnp.broadcast_to(live, (rows, LANES))
        head = jnp.where(live > 0.5, head, 0.0)
        return jnp.concatenate(
            [head.astype(bf16), ref[:, LANES:], live.astype(bf16)], axis=1
        ), live

    own, own_live = cleaned(own_ref)
    peer, _ = cleaned(peer_ref)
    keys = jnp.concatenate([own, peer], axis=0)
    if compact:
        row = lax.broadcasted_iota(jnp.int32, (rows, rows), 0)
        col = lax.broadcasted_iota(jnp.int32, (rows, rows), 1)
        dest = jnp.dot(
            (col < row).astype(bf16), own_live.astype(bf16), preferred_element_type=f32
        )
        slots = lax.broadcasted_iota(jnp.int32, (rows, LANES), 1).astype(f32)
        select = ((dest == slots) & (own_live > 0.5)).astype(bf16)
        query = lax.dot_general(
            select, own, (((0,), (0,)), ((), ())), preferred_element_type=f32
        )
        query_live = query[:, width:]
        query = query[:, :width].astype(bf16)
    else:
        query_live = own_live
        query = own[:, :width]
    scores = lax.dot_general(
        query, keys[:, :width], (((1,), (1,)), ((), ())), preferred_element_type=f32
    )
    weights = jnp.exp(sharpness * (scores - 1.0)).astype(bf16)
    sums = jnp.dot(weights, keys, preferred_element_type=f32)
    numer = sums[:, :width]
    inverse = 1.0 / sums[:, width : width + 1]
    total = jnp.sum(numer * numer, axis=1, keepdims=True)
    scale = inverse * lax.rsqrt(total * (inverse * inverse) + epsilon)
    unit = jnp.where(query_live[:, 0:1] > 0.5, numer * scale, 0.0)
    if last:
        out_ref[...] = unit
        return
    place = places_ref[number : number + 1, :]
    wanted = lax.broadcasted_iota(jnp.int32, (rows, rows), 0)
    choose = (wanted == place).astype(bf16)
    filled = jnp.sum(choose.astype(f32), axis=1, keepdims=True)
    outgoing = jnp.dot(choose, unit.astype(bf16), preferred_element_type=f32)
    out_ref[:, LANES:] = outgoing[:, LANES:].astype(bf16)
    out_ref[:, :LANES] = mark_empty(outgoing[:, :LANES], filled).astype(bf16)


def call(kernel, out, *args):
    spec = pl.BlockSpec(memory_space=pltpu.VMEM)
    return pl.pallas_call(
        kernel, out_shape=out, in_specs=[spec] * len(args), out_specs=spec,
        compiler_params=pltpu.CompilerParams(vmem_limit_bytes=16 * 2**20),
    )(*args)


def swap_pair(values):
    return lax.ppermute(values, "pair", [(0, 1), (1, 0)])


def body(embeddings, moves):
    rows, width = embeddings.shape[2:]
    clusters = lax.axis_size("owner") * lax.axis_size("sub")
    most = rows // clusters
    targets = moves[:, 0, 0, :]
    state = call(
        state_kernel, jax.ShapeDtypeStruct((rows, width), bf16), embeddings[0, 0], targets
    )
    places = call(
        lambda *refs: places_kernel(clusters, most, *refs),
        jax.ShapeDtypeStruct(targets.shape, jnp.int32),
        targets,
    )
    for number in range(PASSES):
        last = number + 1 == PASSES
        peer = swap_pair(state)
        result = call(
            lambda *refs: pass_kernel(number > 0, last, number, *refs),
            jax.ShapeDtypeStruct((rows, width), f32 if last else bf16),
            state,
            peer,
            places,
        )
        if not last:
            state = lax.all_to_all(
                result.reshape(clusters, most, width),
                ("owner", "sub"),
                split_axis=0,
                concat_axis=0,
                tiled=True,
            ).reshape(rows, width)
    return result[None, None]


def solution(mesh):
    placed = (
        P(("groups", "owner", "sub"), "pair", None, None),
        P(None, ("groups", "owner", "sub"), "pair", None),
    )
    return jax.shard_map(
        body,
        mesh=mesh,
        in_specs=placed,
        out_specs=P(("groups", "owner", "sub"), "pair", None, None),
        check_vma=False,
    )
```

```python
import jax
import jax.numpy as jnp
from jax import lax
from jax.experimental import pallas as pl
from jax.experimental.pallas import tpu as pltpu
from jax.sharding import PartitionSpec as P


PASSES = 3
SHARES = 2
LANES = 128
MARK = 2.0


epsilon = 1e-06
sharpness = 6.0

f32 = jnp.float32
bf16 = jnp.bfloat16
i32 = jnp.int32


def offset_of(clusters, step, core):
    return clusters - 1 - 2 * step - (core ^ (step & 1))


def here():
    cluster = lax.axis_index("owner") * lax.axis_size("sub") + lax.axis_index("sub")
    return cluster, lax.axis_index("pair")


def iota(shape, axis):
    return lax.broadcasted_iota(i32, shape, axis)


def mark_empty(head, live):
    return jnp.where((iota(head.shape, 1) == 0) & jnp.logical_not(live), MARK, head)


def state_kernel(emb_ref, moves_ref, out_ref):
    rows = emb_ref.shape[0]
    values = emb_ref[...]
    count = jnp.sum((moves_ref[0:1, :] >= 0).astype(f32), axis=1, keepdims=True)
    live = iota((rows, 1), 0).astype(f32) < count
    total = jnp.sum(values * values, axis=1, keepdims=True)
    unit = jnp.where(live, values * lax.rsqrt(total + epsilon), 0.0)
    out_ref[:, LANES:] = unit[:, LANES:].astype(bf16)
    out_ref[:, :LANES] = mark_empty(unit[:, :LANES], live).astype(bf16)


def places_kernel(clusters, most, own_ref, peer_ref, out_ref):
    lists, rows = own_ref.shape
    cluster, core = here()
    before = (iota((rows, rows), 0) < iota((rows, rows), 1)).astype(bf16)
    for number in range(lists):
        for half, ref in enumerate((own_ref, peer_ref)):
            targets = ref[number : number + 1, :]
            onehot = (iota((clusters, rows), 0) == targets).astype(f32)
            earlier = jnp.dot(onehot.astype(bf16), before, preferred_element_type=f32)
            rank = jnp.sum(onehot * earlier, axis=0, keepdims=True).astype(i32)
            back = clusters - 1 - (targets ^ cluster)
            step = back >> 1
            mine = ((back & 1) ^ (step & 1)) == core
            place = (step * SHARES + (core ^ half)) * most + rank
            out_ref[number : number + 1, half * rows : (half + 1) * rows] = jnp.where(
                (targets >= 0) & mine, place, -1
            )


def pass_kernel(clusters, most, number, last, count, *refs):
    blocks, (places_ref, *outs) = refs[:count], refs[count:]
    width = blocks[0].shape[1]
    total_rows = count * blocks[0].shape[0]
    rows = total_rows // SHARES
    block = SHARES * most
    cluster, core = here()

    heads = jnp.concatenate([ref[:, :LANES] for ref in blocks], axis=0).astype(f32)
    live = jnp.broadcast_to((heads[:, 0:1] < 1.5).astype(f32), (total_rows, LANES))
    heads = jnp.where(live > 0.5, heads, 0.0).astype(bf16)
    tails = jnp.concatenate([ref[:, LANES:] for ref in blocks], axis=0)
    keys = jnp.concatenate([heads, tails], axis=1)
    flags = live.astype(bf16)

    if number == 0:
        place = places_ref[number : number + 1, :]
        select = (iota((rows, total_rows), 0) == place).astype(bf16)
    else:

        def order(index):
            half = (index >= rows).astype(i32)
            inner = index - half * rows
            step = inner // block
            share = (inner // most) & 1
            source = cluster ^ offset_of(clusters, step, core ^ half)
            return share, share * (4 * rows) + source * most + inner % most

        share, key = order(iota((total_rows, 1), 0))
        _, other = order(iota((1, total_rows), 1))
        ahead = key - other
        ahead = ((ahead > 0) & (ahead < 2 * rows)).astype(bf16)
        slot = jnp.dot(ahead, flags, preferred_element_type=f32)
        slot = jnp.where(live > 0.5, slot, -1.0)[:, 0:1]
        lane = iota((total_rows, rows), 1).astype(f32)
        own = (share == core).astype(f32)
        mine = ((slot == lane) & (own > 0.5)).astype(bf16)
        if last:
            wanted = (iota((rows, rows), 0) == iota((rows, rows), 1)).astype(bf16)
        else:
            theirs = ((slot == lane) & (own < 0.5)).astype(bf16)
            mine = jnp.concatenate([mine, theirs], axis=1)
            place = places_ref[number : number + 1, :]
            wanted = (iota((rows, total_rows), 0) == place).astype(bf16)
        select = lax.dot_general(
            wanted, mine, (((1,), (1,)), ((), ())), preferred_element_type=f32
        ).astype(bf16)

    scores = lax.dot_general(keys, keys, (((1,), (1,)), ((), ())), preferred_element_type=f32)
    weights = jnp.exp(sharpness * (scores - 1.0)).astype(bf16)
    chosen = jnp.dot(select, weights, preferred_element_type=f32).astype(bf16)
    sums = jnp.dot(
        chosen, jnp.concatenate([keys, flags], axis=1), preferred_element_type=f32
    )
    numer = sums[:, :width]
    denom = sums[:, width : width + 1]
    found = denom > 0.0
    inverse = 1.0 / jnp.where(found, denom, 1.0)
    total = jnp.sum(numer * numer, axis=1, keepdims=True)
    scale = inverse * lax.rsqrt(total * (inverse * inverse) + epsilon)
    unit = jnp.where(found, numer * scale, 0.0)
    if last:
        outs[0][...] = unit
        return
    head = mark_empty(unit[:, :LANES], found).astype(bf16)
    tail = unit[:, LANES:].astype(bf16)
    size = outs[0].shape[0]
    for index, out in enumerate(outs):
        out[:, :LANES] = head[index * size : (index + 1) * size]
        out[:, LANES:] = tail[index * size : (index + 1) * size]


def call(kernel, out, *args):
    spec = pl.BlockSpec(memory_space=pltpu.VMEM)
    return pl.pallas_call(
        kernel,
        out_shape=out,
        in_specs=[spec] * len(args),
        out_specs=jax.tree.map(lambda _: spec, out),
        compiler_params=pltpu.CompilerParams(vmem_limit_bytes=16 * 2**20),
    )(*args)


def swap_pair(values):
    return lax.ppermute(values, "pair", [(0, 1), (1, 0)])


def send(values, clusters, step):
    pairs = [
        (cluster * 2 + core, (cluster ^ offset_of(clusters, step, core)) * 2 + core)
        for cluster in range(clusters)
        for core in range(2)
    ]
    return lax.ppermute(values, ("owner", "sub", "pair"), pairs)


def body(embeddings, moves):
    rows, width = embeddings.shape[2:]
    clusters = lax.axis_size("owner") * lax.axis_size("sub")
    most = rows // clusters
    steps = clusters // 2
    block = SHARES * most
    aligned = block % 16 == 0
    targets = moves[:, 0, 0, :]
    peer_targets = swap_pair(targets)
    state = call(
        state_kernel, jax.ShapeDtypeStruct((rows, width), bf16), embeddings[0, 0], targets
    )
    places = call(
        lambda *refs: places_kernel(clusters, most, *refs),
        jax.ShapeDtypeStruct((targets.shape[0], SHARES * rows), i32),
        targets,
        peer_targets,
    )
    keys = [state, swap_pair(state)]
    for number in range(PASSES):
        last = number + 1 == PASSES
        if last:
            out = jax.ShapeDtypeStruct((rows, width), f32)
        elif aligned:
            out = [jax.ShapeDtypeStruct((block, width), bf16)] * steps
        else:
            out = [jax.ShapeDtypeStruct((rows, width), bf16)]
        result = call(
            lambda *refs: pass_kernel(clusters, most, number, last, len(keys), *refs),
            out,
            *keys,
            places,
        )
        if last:
            return result[None, None]
        if not aligned:
            result = [result[0][step * block : (step + 1) * block] for step in range(steps)]
        far, near = [], []
        for step in range(steps):
            far.append(send(result[step], clusters, step))
        for step in range(steps):
            near.append(swap_pair(far[step]))
        if aligned:
            keys = far + near
        else:
            keys = [jnp.concatenate(far, axis=0), jnp.concatenate(near, axis=0)]


def solution(mesh):
    placed = (
        P(("groups", "owner", "sub"), "pair", None, None),
        P(None, ("groups", "owner", "sub"), "pair", None),
    )
    return jax.shard_map(
        body,
        mesh=mesh,
        in_specs=placed,
        out_specs=P(("groups", "owner", "sub"), "pair", None, None),
        check_vma=False,
    )
```

```python
import jax
import jax.numpy as jnp
from jax import lax
from jax.experimental import pallas as pl
from jax.experimental.pallas import tpu as pltpu
from jax.sharding import PartitionSpec as P


PASSES = 3
SHARES = 2
LANES = 128
MARK = 2.0


epsilon = 1e-06
sharpness = 6.0

f32 = jnp.float32
bf16 = jnp.bfloat16
i32 = jnp.int32


def offset_of(clusters, step, core):
    return clusters - 1 - 2 * step - (core ^ (step & 1))


def here():
    cluster = lax.axis_index("owner") * lax.axis_size("sub") + lax.axis_index("sub")
    return cluster, lax.axis_index("pair")


def iota(shape, axis):
    return lax.broadcasted_iota(i32, shape, axis)


def mark_empty(head, live):
    return jnp.where((iota(head.shape, 1) == 0) & jnp.logical_not(live), MARK, head)


def unit_rows(values, targets):
    count = jnp.sum((targets >= 0).astype(f32), axis=1, keepdims=True)
    live = iota((values.shape[0], 1), 0).astype(f32) < count
    total = jnp.sum(values * values, axis=1, keepdims=True)
    unit = jnp.where(live, values * lax.rsqrt(total + epsilon), 0.0).astype(bf16)
    flags = jnp.broadcast_to(live.astype(f32), (values.shape[0], LANES)).astype(bf16)
    return unit, flags


def state_kernel(emb_ref, moves_ref, out_ref, flags_ref):
    out_ref[...], flags_ref[...] = unit_rows(emb_ref[...], moves_ref[0:1, :])


def index_kernel(clusters, most, own_ref, peer_ref, wanted_ref, ahead_ref):
    lists, rows = own_ref.shape
    cluster, core = here()
    before = (iota((rows, rows), 0) < iota((rows, rows), 1)).astype(bf16)
    for number in range(lists):
        for half, ref in enumerate((own_ref, peer_ref)):
            targets = ref[number : number + 1, :]
            onehot = (iota((clusters, rows), 0) == targets).astype(f32)
            earlier = jnp.dot(onehot.astype(bf16), before, preferred_element_type=f32)
            rank = jnp.sum(onehot * earlier, axis=0, keepdims=True).astype(i32)
            back = clusters - 1 - (targets ^ cluster)
            step = back >> 1
            mine = ((back & 1) ^ (step & 1)) == core
            place = (step * SHARES + (core ^ half)) * most + rank
            place = jnp.where((targets >= 0) & mine, place, -1)
            wanted_ref[number, :, half * rows : (half + 1) * rows] = (
                iota((rows, rows), 0) == place
            ).astype(bf16)
    _, key = arrival(clusters, most, rows, iota((SHARES * rows, 1), 0))
    _, other = arrival(clusters, most, rows, iota((1, SHARES * rows), 1))
    ahead = key - other
    ahead_ref[...] = ((ahead > 0) & (ahead < 2 * rows)).astype(bf16)


def arrival(clusters, most, rows, index):
    cluster, core = here()
    half = (index >= rows).astype(i32)
    inner = index - half * rows
    step = inner // (SHARES * most)
    share = (inner // most) & 1
    source = cluster ^ offset_of(clusters, step, core ^ half)
    return share, share * (4 * rows) + source * most + inner % most


def pass_kernel(clusters, most, number, last, count, *refs):
    blocks, outs = refs[:count], refs[count + 2 :]
    wanted_ref, ahead_ref = refs[count : count + 2]
    width = blocks[0].shape[1]
    total_rows = ahead_ref.shape[0]
    rows = total_rows // SHARES

    if number == 0:
        state_ref, flags_ref, peer_ref, targets_ref = blocks
        peer, peer_flags = unit_rows(peer_ref[...], targets_ref[0:1, :])
        keys = jnp.concatenate([state_ref[...], peer], axis=0)
        flags = jnp.concatenate([flags_ref[...], peer_flags], axis=0)
        scores = lax.dot_general(keys, keys, (((1,), (1,)), ((), ())), preferred_element_type=f32)
        select = wanted_ref[number]
    else:
        heads = jnp.concatenate([ref[:, :LANES] for ref in blocks], axis=0).astype(f32)
        live = jnp.broadcast_to((heads[:, 0:1] < 1.5).astype(f32), (total_rows, LANES))
        heads = jnp.where(live > 0.5, heads, 0.0).astype(bf16)
        tails = jnp.concatenate([ref[:, LANES:] for ref in blocks], axis=0)
        keys = jnp.concatenate([heads, tails], axis=1)
        flags = live.astype(bf16)
        scores = lax.dot_general(keys, keys, (((1,), (1,)), ((), ())), preferred_element_type=f32)
        _, core = here()
        share, _ = arrival(clusters, most, rows, iota((total_rows, 1), 0))
        slot = jnp.dot(ahead_ref[...], flags, preferred_element_type=f32)
        slot = jnp.where(live > 0.5, slot, -1.0)[:, 0:1]
        lane = iota((total_rows, rows), 1).astype(f32)
        own = (share == core).astype(f32)
        mine = ((slot == lane) & (own > 0.5)).astype(bf16)
        if last:
            wanted = (iota((rows, rows), 0) == iota((rows, rows), 1)).astype(bf16)
        else:
            theirs = ((slot == lane) & (own < 0.5)).astype(bf16)
            mine = jnp.concatenate([mine, theirs], axis=1)
            wanted = wanted_ref[number]
        select = lax.dot_general(
            wanted, mine, (((1,), (1,)), ((), ())), preferred_element_type=f32
        ).astype(bf16)

    weights = jnp.exp(sharpness * (scores - 1.0)).astype(bf16)
    chosen = jnp.dot(select, weights, preferred_element_type=f32).astype(bf16)
    sums = jnp.dot(
        chosen, jnp.concatenate([keys, flags], axis=1), preferred_element_type=f32
    )
    numer = sums[:, :width]
    denom = sums[:, width : width + 1]
    found = denom > 0.0
    inverse = 1.0 / jnp.where(found, denom, 1.0)
    total = jnp.sum(numer * numer, axis=1, keepdims=True)
    scale = inverse * lax.rsqrt(total * (inverse * inverse) + epsilon)
    unit = jnp.where(found, numer * scale, 0.0)
    if last:
        outs[0][...] = unit
        return
    head = mark_empty(unit[:, :LANES], found).astype(bf16)
    tail = unit[:, LANES:].astype(bf16)
    size = outs[0].shape[0]
    for index, out in enumerate(outs):
        out[:, :LANES] = head[index * size : (index + 1) * size]
        out[:, LANES:] = tail[index * size : (index + 1) * size]


def call(kernel, out, *args):
    spec = pl.BlockSpec(memory_space=pltpu.VMEM)
    return pl.pallas_call(
        kernel,
        out_shape=out,
        in_specs=[spec] * len(args),
        out_specs=jax.tree.map(lambda _: spec, out),
        compiler_params=pltpu.CompilerParams(vmem_limit_bytes=16 * 2**20),
    )(*args)


def swap_pair(values):
    return lax.ppermute(values, "pair", [(0, 1), (1, 0)])


def send(values, clusters, step):
    pairs = [
        (cluster * 2 + core, (cluster ^ offset_of(clusters, step, core)) * 2 + core)
        for cluster in range(clusters)
        for core in range(2)
    ]
    return lax.ppermute(values, ("owner", "sub", "pair"), pairs)


def body(embeddings, moves):
    rows, width = embeddings.shape[2:]
    clusters = lax.axis_size("owner") * lax.axis_size("sub")
    most = rows // clusters
    steps = clusters // 2
    block = SHARES * most
    aligned = block % 16 == 0
    targets = moves[:, 0, 0, :]
    values = embeddings[0, 0]
    peer_targets = swap_pair(targets)
    peer_values = swap_pair(values)
    state, flags = call(
        state_kernel,
        [
            jax.ShapeDtypeStruct((rows, width), bf16),
            jax.ShapeDtypeStruct((rows, LANES), bf16),
        ],
        values,
        targets,
    )
    tables = call(
        lambda *refs: index_kernel(clusters, most, *refs),
        [
            jax.ShapeDtypeStruct((targets.shape[0], rows, SHARES * rows), bf16),
            jax.ShapeDtypeStruct((SHARES * rows, SHARES * rows), bf16),
        ],
        targets,
        peer_targets,
    )
    keys = [state, flags, peer_values, peer_targets]
    for number in range(PASSES):
        last = number + 1 == PASSES
        if last:
            out = jax.ShapeDtypeStruct((rows, width), f32)
        elif aligned:
            out = [jax.ShapeDtypeStruct((block, width), bf16)] * steps
        else:
            out = [jax.ShapeDtypeStruct((rows, width), bf16)]
        result = call(
            lambda *refs: pass_kernel(clusters, most, number, last, len(keys), *refs),
            out,
            *keys,
            *tables,
        )
        if last:
            return result[None, None]
        if not aligned:
            result = [result[0][step * block : (step + 1) * block] for step in range(steps)]
        far, near = [], []
        for step in range(steps):
            far.append(send(result[step], clusters, step))
        for step in range(steps):
            near.append(swap_pair(far[step]))
        if aligned:
            keys = far + near
        else:
            keys = [jnp.concatenate(far, axis=0), jnp.concatenate(near, axis=0)]


def solution(mesh):
    placed = (
        P(("groups", "owner", "sub"), "pair", None, None),
        P(None, ("groups", "owner", "sub"), "pair", None),
    )
    return jax.shard_map(
        body,
        mesh=mesh,
        in_specs=placed,
        out_specs=P(("groups", "owner", "sub"), "pair", None, None),
        check_vma=False,
    )
```

```python
import jax
import jax.numpy as jnp
from jax import lax
from jax.experimental import pallas as pl
from jax.experimental.pallas import tpu as pltpu
from jax.sharding import PartitionSpec as P


PASSES = 3
SHARES = 2
LANES = 128
MARK = 2.0
CHUNKS = 4


epsilon = 1e-06
sharpness = 6.0

f32 = jnp.float32
bf16 = jnp.bfloat16
i32 = jnp.int32


def offset_of(clusters, step, core):
    return clusters - 1 - 2 * step - (core ^ (step & 1))


def here():
    cluster = lax.axis_index("owner") * lax.axis_size("sub") + lax.axis_index("sub")
    return cluster, lax.axis_index("pair")


def iota(shape, axis):
    return lax.broadcasted_iota(i32, shape, axis)


def mark_empty(head, live):
    return jnp.where((iota(head.shape, 1) == 0) & jnp.logical_not(live), MARK, head)


def unit_rows(values, targets):
    count = jnp.sum((targets >= 0).astype(f32), axis=1, keepdims=True)
    live = iota((values.shape[0], 1), 0).astype(f32) < count
    total = jnp.sum(values * values, axis=1, keepdims=True)
    unit = jnp.where(live, values * lax.rsqrt(total + epsilon), 0.0).astype(bf16)
    flags = jnp.broadcast_to(live.astype(f32), (values.shape[0], LANES)).astype(bf16)
    return unit, flags


def state_kernel(emb_ref, moves_ref, out_ref, flags_ref):
    out_ref[...], flags_ref[...] = unit_rows(emb_ref[...], moves_ref[0:1, :])


def index_kernel(clusters, most, own_ref, peer_ref, wanted_ref, ahead_ref):
    lists, rows = own_ref.shape
    cluster, core = here()
    before = (iota((rows, rows), 0) < iota((rows, rows), 1)).astype(bf16)
    for number in range(lists):
        for half, ref in enumerate((own_ref, peer_ref)):
            targets = ref[number : number + 1, :]
            onehot = (iota((clusters, rows), 0) == targets).astype(f32)
            earlier = jnp.dot(onehot.astype(bf16), before, preferred_element_type=f32)
            rank = jnp.sum(onehot * earlier, axis=0, keepdims=True).astype(i32)
            back = clusters - 1 - (targets ^ cluster)
            step = back >> 1
            mine = ((back & 1) ^ (step & 1)) == core
            place = (step * SHARES + (core ^ half)) * most + rank
            place = jnp.where((targets >= 0) & mine, place, -1)
            wanted_ref[number, :, half * rows : (half + 1) * rows] = (
                iota((rows, rows), 0) == place
            ).astype(bf16)
    _, key = arrival(clusters, most, rows, iota((SHARES * rows, 1), 0))
    _, other = arrival(clusters, most, rows, iota((1, SHARES * rows), 1))
    ahead = key - other
    ahead_ref[...] = ((ahead > 0) & (ahead < 2 * rows)).astype(bf16)


def arrival(clusters, most, rows, index):
    cluster, core = here()
    half = (index >= rows).astype(i32)
    inner = index - half * rows
    step = inner // (SHARES * most)
    share = (inner // most) & 1
    source = cluster ^ offset_of(clusters, step, core ^ half)
    return share, share * (4 * rows) + source * most + inner % most


def pass_kernel(clusters, most, number, last, count, *refs):
    blocks, outs = refs[:count], refs[count + 2 :]
    wanted_ref, ahead_ref = refs[count : count + 2]
    width = blocks[0].shape[1]
    total_rows = ahead_ref.shape[0]
    rows = total_rows // SHARES

    if number == 0:
        state_ref, flags_ref, peer_ref, targets_ref = blocks
        peer, peer_flags = unit_rows(peer_ref[...], targets_ref[0:1, :])
        keys = jnp.concatenate([state_ref[...], peer], axis=0)
        flags = jnp.concatenate([flags_ref[...], peer_flags], axis=0)
        scores = lax.dot_general(keys, keys, (((1,), (1,)), ((), ())), preferred_element_type=f32)
        select = wanted_ref[number]
    else:
        heads = jnp.concatenate([ref[:, :LANES] for ref in blocks], axis=0).astype(f32)
        live = jnp.broadcast_to((heads[:, 0:1] < 1.5).astype(f32), (total_rows, LANES))
        heads = jnp.where(live > 0.5, heads, 0.0).astype(bf16)
        tails = jnp.concatenate([ref[:, LANES:] for ref in blocks], axis=0)
        keys = jnp.concatenate([heads, tails], axis=1)
        flags = live.astype(bf16)
        rough = jnp.concatenate([ref[...] for ref in blocks], axis=0)
        scores = lax.dot_general(rough, rough, (((1,), (1,)), ((), ())), preferred_element_type=f32)
        _, core = here()
        share, _ = arrival(clusters, most, rows, iota((total_rows, 1), 0))
        slot = jnp.dot(ahead_ref[...], flags, preferred_element_type=f32)
        slot = jnp.where(live > 0.5, slot, -1.0)[:, 0:1]
        lane = iota((total_rows, rows), 1).astype(f32)
        own = (share == core).astype(f32)
        mine = ((slot == lane) & (own > 0.5)).astype(bf16)
        if last:
            wanted = (iota((rows, rows), 0) == iota((rows, rows), 1)).astype(bf16)
        else:
            theirs = ((slot == lane) & (own < 0.5)).astype(bf16)
            mine = jnp.concatenate([mine, theirs], axis=1)
            wanted = wanted_ref[number]
        select = lax.dot_general(
            wanted, mine, (((1,), (1,)), ((), ())), preferred_element_type=f32
        ).astype(bf16)

    weights = jnp.exp(sharpness * (scores - 1.0)).astype(bf16)
    chosen = jnp.dot(select, weights, preferred_element_type=f32).astype(bf16)
    sums = jnp.dot(
        chosen, jnp.concatenate([keys, flags], axis=1), preferred_element_type=f32
    )
    numer = sums[:, :width]
    denom = sums[:, width : width + 1]
    found = denom > 0.0
    inverse = 1.0 / jnp.where(found, denom, 1.0)
    total = jnp.sum(numer * numer, axis=1, keepdims=True)
    scale = inverse * lax.rsqrt(total * (inverse * inverse) + epsilon)
    if last:
        out, staged, done = outs
        size = rows // CHUNKS
        copies = []
        for index in range(CHUNKS):
            part = slice(index * size, (index + 1) * size)
            staged[part] = jnp.where(found[part], numer[part] * scale[part], 0.0)
            copies.append(pltpu.make_async_copy(staged.at[part], out.at[part], done.at[index]))
            copies[-1].start()
        for copy in copies:
            copy.wait()
        return
    unit = jnp.where(found, numer * scale, 0.0)
    head = mark_empty(unit[:, :LANES], found).astype(bf16)
    tail = unit[:, LANES:].astype(bf16)
    size = outs[0].shape[0]
    for index, out in enumerate(outs):
        out[:, :LANES] = head[index * size : (index + 1) * size]
        out[:, LANES:] = tail[index * size : (index + 1) * size]


def call(kernel, out, *args, space=pltpu.VMEM, scratch=()):
    return pl.pallas_call(
        kernel,
        out_shape=out,
        in_specs=[pl.BlockSpec(memory_space=pltpu.VMEM)] * len(args),
        out_specs=jax.tree.map(lambda _: pl.BlockSpec(memory_space=space), out),
        scratch_shapes=scratch,
        compiler_params=pltpu.CompilerParams(vmem_limit_bytes=16 * 2**20),
    )(*args)


def swap_pair(values):
    return lax.ppermute(values, "pair", [(0, 1), (1, 0)])


def send(values, clusters, step):
    pairs = [
        (cluster * 2 + core, (cluster ^ offset_of(clusters, step, core)) * 2 + core)
        for cluster in range(clusters)
        for core in range(2)
    ]
    return lax.ppermute(values, ("owner", "sub", "pair"), pairs)


def body(embeddings, moves):
    rows, width = embeddings.shape[2:]
    clusters = lax.axis_size("owner") * lax.axis_size("sub")
    most = rows // clusters
    steps = clusters // 2
    block = SHARES * most
    aligned = block % 16 == 0
    targets = moves[:, 0, 0, :]
    values = embeddings[0, 0]
    peer_targets = swap_pair(targets)
    peer_values = swap_pair(values)
    state, flags = call(
        state_kernel,
        [
            jax.ShapeDtypeStruct((rows, width), bf16),
            jax.ShapeDtypeStruct((rows, LANES), bf16),
        ],
        values,
        targets,
    )
    tables = call(
        lambda *refs: index_kernel(clusters, most, *refs),
        [
            jax.ShapeDtypeStruct((targets.shape[0], rows, SHARES * rows), bf16),
            jax.ShapeDtypeStruct((SHARES * rows, SHARES * rows), bf16),
        ],
        targets,
        peer_targets,
    )
    keys = [state, flags, peer_values, peer_targets]
    for number in range(PASSES):
        last = number + 1 == PASSES
        if last:
            out = jax.ShapeDtypeStruct((rows, width), f32)
        elif aligned:
            out = [jax.ShapeDtypeStruct((block, width), bf16)] * steps
        else:
            out = [jax.ShapeDtypeStruct((rows, width), bf16)]
        result = call(
            lambda *refs: pass_kernel(clusters, most, number, last, len(keys), *refs),
            out,
            *keys,
            *tables,
            space=pl.ANY if last else pltpu.VMEM,
            scratch=[pltpu.VMEM((rows, width), f32), pltpu.SemaphoreType.DMA((CHUNKS,))]
            if last
            else (),
        )
        if last:
            return result[None, None]
        if not aligned:
            result = [result[0][step * block : (step + 1) * block] for step in range(steps)]
        far, near = [], []
        for step in range(steps):
            far.append(send(result[step], clusters, step))
        for step in range(steps):
            near.append(swap_pair(far[step]))
        if aligned:
            keys = far + near
        else:
            keys = [jnp.concatenate(far, axis=0), jnp.concatenate(near, axis=0)]


def solution(mesh):
    placed = (
        P(("groups", "owner", "sub"), "pair", None, None),
        P(None, ("groups", "owner", "sub"), "pair", None),
    )
    return jax.shard_map(
        body,
        mesh=mesh,
        in_specs=placed,
        out_specs=P(("groups", "owner", "sub"), "pair", None, None),
        check_vma=False,
    )
```

```python
import jax
import jax.numpy as jnp
from jax import lax
from jax.experimental import pallas as pl
from jax.experimental.pallas import tpu as pltpu
from jax.sharding import PartitionSpec as P


PASSES = 3
SHARES = 2
LANES = 128
MARK = 2.0
CHUNKS = 4


epsilon = 1e-06
sharpness = 6.0

f32 = jnp.float32
bf16 = jnp.bfloat16
i32 = jnp.int32


def offset_of(clusters, step, core):
    return clusters - 1 - 2 * step - (core ^ (step & 1))


def here():
    cluster = lax.axis_index("owner") * lax.axis_size("sub") + lax.axis_index("sub")
    return cluster, lax.axis_index("pair")


def iota(shape, axis):
    return lax.broadcasted_iota(i32, shape, axis)


def mark_empty(head, live):
    return jnp.where((iota(head.shape, 1) == 0) & jnp.logical_not(live), MARK, head)


def unit_rows(values, targets):
    count = jnp.sum((targets >= 0).astype(f32), axis=1, keepdims=True)
    live = iota((values.shape[0], 1), 0).astype(f32) < count
    total = jnp.sum(values * values, axis=1, keepdims=True)
    unit = jnp.where(live, values * lax.rsqrt(total + epsilon), 0.0).astype(bf16)
    flags = jnp.broadcast_to(live.astype(f32), (values.shape[0], LANES)).astype(bf16)
    return unit, flags


def state_kernel(emb_ref, moves_ref, out_ref, flags_ref):
    out_ref[...], flags_ref[...] = unit_rows(emb_ref[...], moves_ref[0:1, :])


def index_kernel(clusters, most, own_ref, peer_ref, wanted_ref, ahead_ref):
    lists, rows = own_ref.shape
    cluster, core = here()
    before = (iota((rows, rows), 0) < iota((rows, rows), 1)).astype(bf16)
    for number in range(lists):
        for half, ref in enumerate((own_ref, peer_ref)):
            targets = ref[number : number + 1, :]
            onehot = (iota((clusters, rows), 0) == targets).astype(f32)
            earlier = jnp.dot(onehot.astype(bf16), before, preferred_element_type=f32)
            rank = jnp.sum(onehot * earlier, axis=0, keepdims=True).astype(i32)
            back = clusters - 1 - (targets ^ cluster)
            step = back >> 1
            mine = ((back & 1) ^ (step & 1)) == core
            place = (step * SHARES + (core ^ half)) * most + rank
            place = jnp.where((targets >= 0) & mine, place, -1)
            wanted_ref[number, :, half * rows : (half + 1) * rows] = (
                iota((rows, rows), 0) == place
            ).astype(bf16)
    _, key = arrival(clusters, most, rows, iota((SHARES * rows, 1), 0))
    _, other = arrival(clusters, most, rows, iota((1, SHARES * rows), 1))
    ahead = key - other
    ahead_ref[...] = ((ahead > 0) & (ahead < 2 * rows)).astype(bf16)


def arrival(clusters, most, rows, index):
    cluster, core = here()
    half = (index >= rows).astype(i32)
    inner = index - half * rows
    step = inner // (SHARES * most)
    share = (inner // most) & 1
    source = cluster ^ offset_of(clusters, step, core ^ half)
    return share, share * (4 * rows) + source * most + inner % most


def pass_kernel(clusters, most, number, last, count, *refs):
    blocks, outs = refs[:count], refs[count + 2 :]
    wanted_ref, ahead_ref = refs[count : count + 2]
    width = blocks[0].shape[1]
    total_rows = ahead_ref.shape[0]
    rows = total_rows // SHARES

    if number == 0:
        state_ref, flags_ref, peer_ref, targets_ref = blocks
        peer, peer_flags = unit_rows(peer_ref[...], targets_ref[0:1, :])
        keys = jnp.concatenate([state_ref[...], peer], axis=0)
        flags = jnp.concatenate([flags_ref[...], peer_flags], axis=0)
        scores = lax.dot_general(keys, keys, (((1,), (1,)), ((), ())), preferred_element_type=f32)
        select = wanted_ref[number]
    else:
        heads = jnp.concatenate([ref[:, :LANES] for ref in blocks], axis=0).astype(f32)
        live = jnp.broadcast_to((heads[:, 0:1] < 1.5).astype(f32), (total_rows, LANES))
        heads = jnp.where(live > 0.5, heads, 0.0).astype(bf16)
        tails = jnp.concatenate([ref[:, LANES:] for ref in blocks], axis=0)
        keys = jnp.concatenate([heads, tails], axis=1)
        flags = live.astype(bf16)
        rough = jnp.concatenate([ref[...] for ref in blocks], axis=0)
        cut = width // (4 * LANES) * 2 * LANES + LANES
        scores = sum(
            lax.dot_general(part, part, (((1,), (1,)), ((), ())), preferred_element_type=f32)
            for part in (rough[:, :cut], rough[:, cut:])
        )
        _, core = here()
        share, _ = arrival(clusters, most, rows, iota((total_rows, 1), 0))
        slot = jnp.dot(ahead_ref[...], flags, preferred_element_type=f32)
        slot = jnp.where(live > 0.5, slot, -1.0)[:, 0:1]
        lane = iota((total_rows, rows), 1).astype(f32)
        own = (share == core).astype(f32)
        mine = ((slot == lane) & (own > 0.5)).astype(bf16)
        if last:
            wanted = (iota((rows, rows), 0) == iota((rows, rows), 1)).astype(bf16)
        else:
            theirs = ((slot == lane) & (own < 0.5)).astype(bf16)
            mine = jnp.concatenate([mine, theirs], axis=1)
            wanted = wanted_ref[number]
        select = lax.dot_general(
            wanted, mine, (((1,), (1,)), ((), ())), preferred_element_type=f32
        ).astype(bf16)

    weights = jnp.exp(sharpness * (scores - 1.0)).astype(bf16)
    chosen = jnp.dot(select, weights, preferred_element_type=f32).astype(bf16)
    sums = jnp.dot(
        chosen, jnp.concatenate([keys, flags], axis=1), preferred_element_type=f32
    )
    numer = sums[:, :width]
    denom = sums[:, width : width + 1]
    found = denom > 0.0
    inverse = 1.0 / jnp.where(found, denom, 1.0)
    total = jnp.sum(numer * numer, axis=1, keepdims=True)
    scale = inverse * lax.rsqrt(total * (inverse * inverse) + epsilon)
    if last:
        out, staged, done = outs
        size = rows // CHUNKS
        copies = []
        for index in range(CHUNKS):
            part = slice(index * size, (index + 1) * size)
            staged[part] = jnp.where(found[part], numer[part] * scale[part], 0.0)
            copies.append(pltpu.make_async_copy(staged.at[part], out.at[part], done.at[index]))
            copies[-1].start()
        for copy in copies:
            copy.wait()
        return
    unit = jnp.where(found, numer * scale, 0.0)
    head = mark_empty(unit[:, :LANES], found).astype(bf16)
    tail = unit[:, LANES:].astype(bf16)
    size = outs[0].shape[0]
    for index, out in enumerate(outs):
        out[:, :LANES] = head[index * size : (index + 1) * size]
        out[:, LANES:] = tail[index * size : (index + 1) * size]


def call(kernel, out, *args, space=pltpu.VMEM, scratch=()):
    return pl.pallas_call(
        kernel,
        out_shape=out,
        in_specs=[pl.BlockSpec(memory_space=pltpu.VMEM)] * len(args),
        out_specs=jax.tree.map(lambda _: pl.BlockSpec(memory_space=space), out),
        scratch_shapes=scratch,
        compiler_params=pltpu.CompilerParams(vmem_limit_bytes=16 * 2**20),
    )(*args)


def swap_pair(values):
    return lax.ppermute(values, "pair", [(0, 1), (1, 0)])


def send(values, clusters, step):
    pairs = [
        (cluster * 2 + core, (cluster ^ offset_of(clusters, step, core)) * 2 + core)
        for cluster in range(clusters)
        for core in range(2)
    ]
    return lax.ppermute(values, ("owner", "sub", "pair"), pairs)


def body(embeddings, moves):
    rows, width = embeddings.shape[2:]
    clusters = lax.axis_size("owner") * lax.axis_size("sub")
    most = rows // clusters
    steps = clusters // 2
    block = SHARES * most
    aligned = block % 16 == 0
    targets = moves[:, 0, 0, :]
    values = embeddings[0, 0]
    peer_targets = swap_pair(targets)
    peer_values = swap_pair(values)
    state, flags = call(
        state_kernel,
        [
            jax.ShapeDtypeStruct((rows, width), bf16),
            jax.ShapeDtypeStruct((rows, LANES), bf16),
        ],
        values,
        targets,
    )
    tables = call(
        lambda *refs: index_kernel(clusters, most, *refs),
        [
            jax.ShapeDtypeStruct((targets.shape[0], rows, SHARES * rows), bf16),
            jax.ShapeDtypeStruct((SHARES * rows, SHARES * rows), bf16),
        ],
        targets,
        peer_targets,
    )
    keys = [state, flags, peer_values, peer_targets]
    for number in range(PASSES):
        last = number + 1 == PASSES
        if last:
            out = jax.ShapeDtypeStruct((rows, width), f32)
        elif aligned:
            out = [jax.ShapeDtypeStruct((block, width), bf16)] * steps
        else:
            out = [jax.ShapeDtypeStruct((rows, width), bf16)]
        result = call(
            lambda *refs: pass_kernel(clusters, most, number, last, len(keys), *refs),
            out,
            *keys,
            *tables,
            space=pl.ANY if last else pltpu.VMEM,
            scratch=[pltpu.VMEM((rows, width), f32), pltpu.SemaphoreType.DMA((CHUNKS,))]
            if last
            else (),
        )
        if last:
            return result[None, None]
        if not aligned:
            result = [result[0][step * block : (step + 1) * block] for step in range(steps)]
        far, near = [], []
        for step in range(steps):
            far.append(send(result[step], clusters, step))
        for step in range(steps):
            near.append(swap_pair(far[step]))
        if aligned:
            keys = far + near
        else:
            keys = [jnp.concatenate(far, axis=0), jnp.concatenate(near, axis=0)]


def solution(mesh):
    placed = (
        P(("groups", "owner", "sub"), "pair", None, None),
        P(None, ("groups", "owner", "sub"), "pair", None),
    )
    return jax.shard_map(
        body,
        mesh=mesh,
        in_specs=placed,
        out_specs=P(("groups", "owner", "sub"), "pair", None, None),
        check_vma=False,
    )
```
